32 devices in a mesh: draws: 2 (over y), dst: 4 (over z), org: 2 (over x), st: 2 (over core).
Axes of the slice: x: 2, y: 2, z: 4, core: 2. Of those that a mesh axis runs over, the one named last changes fastest.
Arguments:
- value_now: float32 [8, 2, 64, 4096], P(('draws', 'dst'), 'org', None, 'st'), parts along dimension 0, may hold values from -90 to 490
- utility: float32 [8, 2, 64, 4096], P(('draws', 'dst'), 'org', None, 'st'), parts along dimension 0, may hold values from -6 to 6
- move_costs: float32 [8, 2, 64, 4, 128], P('draws', 'org', None, 'dst'), parts along dimension 0, may hold values from 0 to 3
- dest_blocks: int32 [8, 3], replicated, may hold values from 0 to 7, all different within a row
- row_counts: int32 [8], replicated, may hold values from 1 to 3, as said below
- transition: int32 [4096], replicated, may hold values from 0 to 4095
Outputs:
- value_next: float32 [8, 2, 64, 4096], P(('draws', 'dst'), 'org', None, 'st'), parts along dimension 0
The draws below stay inside these ranges and needn't reach their ends.
There are 2 independent parts, one for each index of `draws`. The reference program is written for one: setup_inputs(seed, part) draws one part's arguments, and reference() takes and returns one part's arrays. A program takes and returns all parts, laid end to end along the dimension named above; an argument that names none is the same for every part. Nothing has to cross between parts.
Inputs may be any that keep to these rules, and one draw needn't show every extreme that they name: `dest_blocks`: each row names 3 different blocks; only the first row_counts[o] of row o count. `row_counts`: some anchor block has 3.
All inputs are finite; a program needn't handle non-finite values.
Results may differ from the reference program's by a relative error of at most 0.00095.
Values may be sent and summed in bfloat16 or wider, within the bound.
No kernel may reach another device: no remote copies, remote signals or barrier semaphores. Data moves between devices by JAX's collectives and lax.ppermute only.
A program may use at most 64 MiB of HBM per device.

```python
import jax
import jax.numpy as jnp
from jax import lax

S = 4096
BLK = 64
DEST_SHARDS = 4
ORIG_SHARDS = 2
NBLK = 8
NNZ = 3
LOCATIONS = 512


def draw_value_now(key, part):
    first_key = jax.random.fold_in(key, 0)
    shape_full = (DEST_SHARDS, ORIG_SHARDS, BLK, S)
    rough = jax.random.normal(first_key, shape_full, jnp.float32)
    drawn = 2.0 * rough
    return jnp.clip(drawn, -90.0, 490.0)


def draw_row_counts(key, part):
    first_key, second_key = jax.random.split(jax.random.fold_in(key, 11))
    counts_drawn = jax.random.randint(first_key, (NBLK,), 1, NNZ + 1, dtype=jnp.int32)
    fullest = jax.random.randint(second_key, (), 0, NBLK, dtype=jnp.int32)
    return counts_drawn.at[fullest].set(NNZ)


def place_ends(result, own_key, smallest, top_value):
    index_at = [jax.random.randint(jax.random.fold_in(own_key, axis), (), 0, length) for axis, length in enumerate(result.shape)]
    widest = result.shape.index(max(result.shape))
    neighbour = index_at[:widest] + [(index_at[widest] + 1) % result.shape[widest]] + index_at[widest + 1:]
    return result.at[tuple(index_at)].set(smallest).at[tuple(neighbour)].set(top_value)


def shard_levels(stream_key, extent, shards, least, largest):
    def one(axis_at, shards_of):
        steps = jax.random.uniform(jax.random.fold_in(jax.random.fold_in(stream_key, 6), axis_at), (shards_of,), jnp.float32, least / len(shards), largest / len(shards))
        return jnp.repeat(jnp.exp(steps), extent[axis_at] // shards_of).reshape((-1,) + (1,) * (len(extent) - axis_at - 1))

    factor_of = one(*shards[0])
    for cut in shards[1:]:
        factor_of = factor_of * one(*cut)
    return factor_of


def different_ones(own_key, rows, count, top, lift):
    ranking = jax.random.permutation(jax.random.fold_in(own_key, 1), count)
    pull = ranking
    for power in range(3):
        pull = pull * pull // count
    pull = pull * lift // count
    lots = jax.random.randint(jax.random.fold_in(own_key, 2), (rows, count), 0, 4096) + pull
    sure = jax.random.permutation(jax.random.fold_in(own_key, 3), rows)[jnp.arange(count) % rows]
    lots = jnp.where(jnp.arange(rows)[:, None] == sure[None, :], 1 << 14, lots)
    score = lots * count + jnp.arange(count)
    return lax.top_k(score.astype(jnp.int32), top)[1].astype(jnp.int32)


def scatter_about(own_key, shape, scale, limit, cuts=(), held_as=jnp.bfloat16):
    loudness = shard_levels(own_key, shape, cuts, -0.22, 0.18) if cuts else 1.0
    values = jax.random.normal(own_key, shape, jnp.float32) * scale * loudness
    return jnp.minimum(jnp.maximum(values, -limit), limit).astype(held_as)


def setup_inputs(seed: int = 0, part: int = 0) -> dict:
    arg_keys = jax.random.split(jax.random.key(seed), 7)
    own_keys = jax.random.split(jax.random.fold_in(arg_keys[6], part), 7)
    value_now = draw_value_now(jax.random.fold_in(jax.random.fold_in(arg_keys[6], part), 71), part)
    utility = scatter_about(own_keys[1], (DEST_SHARDS, ORIG_SHARDS, BLK, S), 1.0, 6.0, ((0, 4), (1, 2), (3, 2)), jnp.float32)
    move_costs = jnp.clip(3.0 * jax.random.uniform(own_keys[2], (DEST_SHARDS, ORIG_SHARDS, BLK, DEST_SHARDS, ORIG_SHARDS * BLK), jnp.float32) ** shard_levels(own_keys[2], (DEST_SHARDS, ORIG_SHARDS, BLK, DEST_SHARDS, ORIG_SHARDS * BLK), ((1, 2), (3, 4)), -0.2, 0.2), 0.0, 3.0)
    dest_blocks = different_ones(arg_keys[3], NBLK, NBLK, NNZ, 6144)
    row_counts = draw_row_counts(jax.random.fold_in(arg_keys[6], 71), part)
    transition = place_ends(jax.random.randint(arg_keys[5], (S,), 0, S), jax.random.fold_in(arg_keys[5], 1), 0, S - 1).astype(jnp.int32)
    return {"value_now": value_now, "utility": utility, "move_costs": move_costs, "dest_blocks": dest_blocks, "row_counts": row_counts, "transition": transition}


DISCOUNT = 0.95
FLOOR = -1.0e30


def reference(value_now, utility, move_costs, dest_blocks, row_counts, transition):
    shifted = jnp.take(value_now.reshape(LOCATIONS, S), transition, axis=1)
    by_block = shifted.reshape(NBLK, BLK, S)
    cost_blocks = move_costs.reshape(NBLK, BLK, NBLK, BLK)
    slot_ids = jnp.arange(NNZ, dtype=jnp.int32)
    group_ids = jnp.arange(DEST_SHARDS, dtype=jnp.int32)

    def anchor_block(anchor):
        listed = dest_blocks[anchor]
        usable = slot_ids < row_counts[anchor]
        dest_rows = by_block[listed]
        block_top = jnp.max(dest_rows, axis=1)
        ceiling = jnp.max(jnp.where(usable[:, None], block_top, FLOOR), axis=0)
        weights = jnp.where(usable[:, None, None], jnp.exp(dest_rows - ceiling[None, None, :]), 0.0).astype(jnp.bfloat16)
        kernel = jnp.exp(-cost_blocks[anchor][:, listed, :]).astype(jnp.bfloat16)
        products = jnp.einsum("inj,njs->nis", kernel.astype(jnp.float32), weights.astype(jnp.float32))
        group_of = listed // ORIG_SHARDS
        group_table = (group_of[:, None] == group_ids[None, :]).astype(jnp.float32)
        partial_value = jnp.einsum("nis,nk->kis", products, group_table, precision=lax.Precision.HIGHEST).astype(jnp.bfloat16)
        merged = jnp.sum(partial_value.astype(jnp.float32), axis=0)
        return ceiling, merged

    ceilings, merged_all = lax.map(anchor_block, jnp.arange(NBLK, dtype=jnp.int32))
    value_next = utility.reshape(NBLK, BLK, S) + DISCOUNT * (ceilings[:, None, :] + jnp.log(merged_all))
    return value_next.reshape(DEST_SHARDS, ORIG_SHARDS, BLK, S)
```

```python
import functools

import jax
import jax.numpy as jnp
from jax import lax
from jax.experimental import pallas as pl
from jax.experimental.pallas import tpu as pltpu
from jax.sharding import PartitionSpec as P

DISCOUNT = 0.95
FLOOR = -1e30
LANES = 128
CHUNKS = 1


def rows_to_lanes(block, first, count):
    return jnp.concatenate([block[first + i : first + i + 1, :] for i in range(count)], axis=1)


def lanes_to_rows(row, rows):
    count = row.shape[1] // LANES
    parts = [row[:, i * LANES : (i + 1) * LANES] for i in range(count)]
    if rows > count:
        parts.append(jnp.zeros((rows - count, LANES), row.dtype))
    return jnp.concatenate(parts, axis=0)


def place(high, low):
    d = lax.axis_index("dst")
    return d // low, d % low


def weigh_kernel(high, low, orig, widths, value_ref, cost_ref, *out_refs):
    plain_refs, keyed_refs, own_ref = out_refs[: len(widths)], out_refs[len(widths) : -1], out_refs[-1]
    my_high, my_low = place(high, low)
    my_orig = lax.axis_index("org")
    rows = value_ref.shape[0]
    cols = cost_ref.shape[2]

    def kernel_part(turn):
        target = (my_low + low - turn) % low
        parts = []
        for r in range(high):
            k = jnp.exp(-cost_ref[((my_high + r) % high) * low + target])
            turned = k
            for s in range(1, orig):
                turned = jnp.where(my_orig == s, pltpu.roll(k, cols - s * rows, 1), turned)
            parts.append(turned.astype(jnp.bfloat16))
        return parts

    for r, part in enumerate(kernel_part(0)):
        own_ref[:, r * cols : (r + 1) * cols] = part
    for turn in range(1, low):
        for r, part in enumerate(kernel_part(turn)):
            keyed_refs[turn - 1][:, r * cols : (r + 1) * cols] = part
    base = high * cols
    start = 0
    tops = []
    for c, width in enumerate(widths):
        v = value_ref[:, start : start + width]
        top = jnp.max(v, axis=0, keepdims=True).astype(jnp.bfloat16).astype(jnp.float32)
        tops.append(top)
        e = jnp.exp(v - top).astype(jnp.bfloat16)
        plain_refs[c][:, :width] = e
        if c == 0:
            for ref in keyed_refs:
                ref[:, base : base + width] = e
        start += width
    packed = lanes_to_rows(jnp.concatenate(tops, axis=1), rows).astype(jnp.bfloat16)
    plain_refs[0][:, widths[0] :] = packed
    for ref in keyed_refs:
        ref[:, base + widths[0] :] = packed


def weigh(high, low, orig, widths, value, cost):
    rows, states = value.shape
    base = high * cost.shape[2]
    shapes = [jax.ShapeDtypeStruct((rows, w + (LANES if c == 0 else 0)), jnp.bfloat16) for c, w in enumerate(widths)]
    shapes += [jax.ShapeDtypeStruct((rows, base + widths[0] + LANES), jnp.bfloat16)] * (low - 1)
    shapes += [jax.ShapeDtypeStruct((rows, base), jnp.bfloat16)]
    return pl.pallas_call(
        functools.partial(weigh_kernel, high, low, orig, widths),
        out_shape=shapes,
        cost_estimate=pl.CostEstimate(
            flops=4 * rows * states, bytes_accessed=8 * rows * states, transcendentals=rows * states
        ),
        name="weigh",
    )(value, cost)


def sums_kernel(high, low, orig, slots, chunk, widths, skips, turns, count_ref, list_ref, *refs):
    groups = low * orig
    rows = refs[0].shape[0]
    key_refs, top_refs = refs[:low], refs[low : low + groups]
    piece_refs, out_refs = refs[low + groups : low + 2 * groups], refs[low + 2 * groups :]
    width = widths[chunk]
    first = sum(widths[:chunk]) // LANES
    my_high, my_low = place(high, low)
    my_orig = lax.axis_index("org")
    tops = [ref[...].astype(jnp.float32) for ref in top_refs]
    for n, turn in enumerate(turns):
        anchor = (((my_high + turn) % high) * low + my_low) * orig + my_orig
        limit = count_ref[anchor]
        feasible = []
        for i in range(low):
            for j in range(orig):
                block = (my_high * low + (my_low + i) % low) * orig + (my_orig + j) % orig

                def hit(k, found):
                    return found | jnp.where((list_ref[anchor, k] == block) & (k < limit), 1, 0)

                feasible.append(lax.fori_loop(0, slots, hit, jnp.int32(0), unroll=slots <= 4) > 0)
        ceiling = functools.reduce(
            jnp.maximum, [jnp.where(f, t, FLOOR) for f, t in zip(feasible, tops)]
        )
        total = jnp.zeros((rows, width), jnp.float32)
        for i in range(low):
            for j in range(orig):
                b = i * orig + j
                scale = jnp.exp(jnp.where(feasible[b], tops[b] - ceiling, FLOOR))
                at = (turn * orig + j) * rows
                product = jnp.dot(
                    key_refs[i][:, at : at + rows],
                    piece_refs[b][:, skips[b] : skips[b] + width],
                    preferred_element_type=jnp.float32,
                )
                total += rows_to_lanes(scale, first, width // LANES) * product
        out_refs[n][:, :width] = total.astype(jnp.bfloat16)
        if chunk == 0:
            out_refs[n][:, width:] = ceiling.astype(jnp.bfloat16)


def sums(high, low, orig, chunk, widths, turns, row_counts, dest_blocks, own_key, gathered):
    rows = own_key.shape[0]
    base = own_key.shape[1]
    groups = low * orig
    smem = pl.BlockSpec(memory_space=pltpu.SMEM)
    keyed = [b // orig > 0 and b % orig == 0 for b in range(groups)]
    width = widths[chunk]
    args, specs = [row_counts, dest_blocks, own_key], [smem, smem, pl.BlockSpec((rows, base), lambda g: (0, 0))]
    skips = [base if chunk == 0 and k else 0 for k in keyed]
    for i in range(1, low):
        args.append(gathered[0][i * orig])
        specs.append(pl.BlockSpec((rows, base), lambda g: (0, 0)))
    for b in range(groups):
        at = (widths[0] + (base if keyed[b] else 0)) // LANES
        args.append(gathered[0][b])
        specs.append(pl.BlockSpec((rows, LANES), functools.partial(lambda at, g: (0, at), at)))
    for b in range(groups):
        args.append(gathered[chunk][b])
        specs.append(pl.BlockSpec(gathered[chunk][b].shape, lambda g: (0, 0)))
    extra = LANES if chunk == 0 else 0
    return pl.pallas_call(
        functools.partial(sums_kernel, high, low, orig, dest_blocks.shape[1], chunk, widths, skips, turns),
        grid=(1,),
        in_specs=specs,
        out_specs=[pl.BlockSpec((rows, width + extra), lambda g: (0, 0))] * len(turns),
        out_shape=[jax.ShapeDtypeStruct((rows, width + extra), jnp.bfloat16)] * len(turns),
        cost_estimate=pl.CostEstimate(
            flops=2 * rows * rows * width * groups * len(turns),
            bytes_accessed=2 * rows * width * (groups + len(turns)),
            transcendentals=groups * width,
        ),
        name="sums",
    )(*args)


def finish_kernel(high, halves, widths, low_size, tile, utility_ref, next_ref, *refs):
    out_ref = refs[-1]
    chunks = len(widths)
    rows, states = utility_ref.shape
    mine = lax.axis_index("st")

    def source(r, h):
        return refs[(r * halves + h) * chunks : (r * halves + h + 1) * chunks]

    pieces = states // low_size
    lefts = []
    tops = []
    for r in range(high):
        stack = []
        rows_of = []
        for h in range(halves):
            got = source(r, h)
            c = got[0][:, widths[0] :].astype(jnp.float32)
            for k in range(pieces):
                at = k * low_size
                chunk = 0
                while at >= widths[chunk]:
                    at -= widths[chunk]
                    chunk += 1
                stack.append(got[chunk][:, at : at + low_size])
                per = low_size // LANES
                rows_of.append(rows_to_lanes(c, k * per, per))
        lefts.append(jnp.concatenate(stack, axis=0))
        tops.append(jnp.concatenate(rows_of, axis=0).astype(jnp.bfloat16))
    for start in range(0, states, tile):
        nxt = next_ref[:, start : start + tile]
        high_part = nxt // low_size
        low_part = nxt % low_size
        onehot = jnp.where(
            lax.broadcasted_iota(jnp.int32, (low_size, tile), 0) == low_part, 1.0, 0.0
        ).astype(jnp.bfloat16)
        values, ceilings = [], []
        for r in range(high):
            every = jnp.dot(lefts[r], onehot, preferred_element_type=jnp.float32)
            every_top = jnp.dot(tops[r], onehot, preferred_element_type=jnp.float32)
            value = jnp.zeros((rows, tile), jnp.float32)
            ceiling = jnp.zeros((1, tile), jnp.float32)
            for h in range(halves):
                part = ((mine + h) % halves) * pieces
                for k in range(pieces):
                    n = h * pieces + k
                    here = high_part == part + k
                    value = jnp.where(here, every[n * rows : (n + 1) * rows, :], value)
                    ceiling = jnp.where(here, every_top[n : n + 1, :], ceiling)
            values.append(value)
            ceilings.append(ceiling)
        ceiling = functools.reduce(jnp.maximum, ceilings)
        merged = sum(v * jnp.exp(c - ceiling) for v, c in zip(values, ceilings))
        out_ref[:, start : start + tile] = utility_ref[:, start : start + tile] + DISCOUNT * (
            ceiling + jnp.log(merged)
        )


def finish(high, halves, widths, utility, chosen, sources):
    rows, states = utility.shape
    low_size = min(512, states)
    tile = min(512, states)
    flat = [a for per_turn in sources for per_half in per_turn for a in per_half]
    return pl.pallas_call(
        functools.partial(finish_kernel, high, halves, widths, low_size, tile),
        out_shape=jax.ShapeDtypeStruct((rows, states), jnp.float32),
        cost_estimate=pl.CostEstimate(
            flops=2 * rows * halves * states * states * high // 1,
            bytes_accessed=8 * rows * states,
            transcendentals=2 * rows * states,
        ),
        name="finish",
    )(utility, chosen, *flat)


def on_device(sizes, value_now, utility, move_costs, dest_blocks, row_counts, transition):
    dest, orig, halves = sizes
    low = 2 if dest % 2 == 0 else 1
    high = dest // low
    rows, states = value_now.shape[2:]
    widths = (states // CHUNKS,) * CHUNKS
    both = ("dst", "org")

    def index(h, l, o):
        return (h * low + l) * orig + o

    def gather(x, i, j):
        pairs = [
            (index(h, l, o), index(h, (l - i) % low, (o - j) % orig))
            for h in range(high)
            for l in range(low)
            for o in range(orig)
        ]
        return lax.ppermute(x, both, pairs)

    def onward(x, r):
        return lax.ppermute(x, "dst", [(h * low + l, ((h + r) % high) * low + l) for h in range(high) for l in range(low)])

    def across(x, h):
        return lax.ppermute(x, "st", [(s, (s - h) % halves) for s in range(halves)])

    cost = move_costs.reshape(move_costs.shape[0], rows, move_costs.shape[4])
    made = weigh(high, low, orig, widths, value_now.reshape(rows, states), cost)
    plain, keyed, own_key = made[:CHUNKS], made[CHUNKS:-1], made[-1]
    gathered = []
    for c in range(CHUNKS):
        row = []
        for i in range(low):
            for j in range(orig):
                x = keyed[i - 1] if c == 0 and i > 0 and j == 0 else plain[c]
                row.append(x if i == j == 0 else gather(x, i, j))
        gathered.append(row)
    step = functools.partial(sums, high, low, orig)
    rest = (row_counts, dest_blocks, own_key, gathered)
    local = [[None] * CHUNKS for _ in range(high)]
    for c in range(CHUNKS):
        if high > 1:
            sent = step(c, widths, tuple(range(1, high)), *rest)
            for r in range(1, high):
                local[r][c] = onward(sent[r - 1], r)
    for c in range(CHUNKS):
        local[0][c] = step(c, widths, (0,), *rest)[0]
    sources = [
        [[x if h == 0 else across(x, h) for x in local[r]] for h in range(halves)] for r in range(high)
    ]
    chosen = lax.dynamic_slice_in_dim(transition, lax.axis_index("st") * states, states).reshape(1, states)
    out = finish(high, halves, widths, utility.reshape(rows, states), chosen, sources)
    return out.reshape(value_now.shape)


def solution(mesh):
    sizes = (mesh.shape["dst"], mesh.shape["org"], mesh.shape["st"])
    return jax.shard_map(
        functools.partial(on_device, sizes),
        mesh=mesh,
        in_specs=(
            P(("draws", "dst"), "org", None, "st"),
            P(("draws", "dst"), "org", None, "st"),
            P("draws", "org", None, "dst", None),
            P(),
            P(),
            P(),
        ),
        out_specs=P(("draws", "dst"), "org", None, "st"),
        check_vma=False,
    )
```

```python
import functools

import jax
import jax.numpy as jnp
from jax import lax
from jax.experimental import pallas as pl
from jax.experimental.pallas import tpu as pltpu
from jax.sharding import PartitionSpec as P


DISCOUNT = 0.95
FLOOR = -1e30
LANES = 128
CHUNKS = 2
LOW_BITS = 9
GRANT = 24 * 2**20
TILES = 4


def call(kernel, outs, flops, touched, args, smem=()):
    specs = [pl.BlockSpec(memory_space=pltpu.SMEM if n in smem else pltpu.VMEM) for n in range(len(args))]
    held = [a if n in smem else pltpu.with_memory_space_constraint(a, pltpu.VMEM) for n, a in enumerate(args)]
    return pl.pallas_call(
        kernel,
        in_specs=specs,
        out_specs=[pl.BlockSpec(memory_space=pltpu.VMEM)] * len(outs),
        out_shape=[pltpu.VMEM(shape, dtype) for shape, dtype in outs],
        compiler_params=pltpu.CompilerParams(vmem_limit_bytes=GRANT),
        cost_estimate=pl.CostEstimate(flops=flops, bytes_accessed=touched, transcendentals=0),
    )(*held)


def rows_to_lanes(block, first, count):
    return jnp.concatenate([block[first + i : first + i + 1, :] for i in range(count)], axis=1)


def lanes_to_rows(row, rows):
    count = row.shape[1] // LANES
    parts = [row[:, i * LANES : (i + 1) * LANES] for i in range(count)]
    if rows > count:
        parts.append(jnp.zeros((rows - count, LANES), row.dtype))
    return jnp.concatenate(parts, axis=0)


def place(low):
    d = lax.axis_index("dst")
    return d // low, d % low


def weigh_kernel(high, low, orig, widths, value_ref, cost_ref, *out_refs):
    plain_refs, keyed_refs, own_ref = out_refs[: len(widths)], out_refs[len(widths) : -1], out_refs[-1]
    my_high, my_low = place(low)
    my_orig = lax.axis_index("org")
    rows = value_ref.shape[0]
    cols = cost_ref.shape[2]

    def kernel_part(turn):
        target = (my_low + low - turn) % low
        parts = []
        for r in range(high):
            k = jnp.exp(-cost_ref[((my_high + r) % high) * low + target])
            turned = k
            for s in range(1, orig):
                turned = jnp.where(my_orig == s, pltpu.roll(k, cols - s * rows, 1), turned)
            parts.append(turned.astype(jnp.bfloat16))
        return parts

    for r, part in enumerate(kernel_part(0)):
        own_ref[:, r * cols : (r + 1) * cols] = part
    for turn in range(1, low):
        for r, part in enumerate(kernel_part(turn)):
            keyed_refs[turn - 1][:, r * cols : (r + 1) * cols] = part
    base = high * cols
    start = 0
    tops = []
    for c, width in enumerate(widths):
        v = value_ref[:, start : start + width]
        top = jnp.max(v, axis=0, keepdims=True).astype(jnp.bfloat16).astype(jnp.float32)
        tops.append(top)
        e = jnp.exp(v - top).astype(jnp.bfloat16)
        plain_refs[c][:, :width] = e
        if c == 0:
            for ref in keyed_refs:
                ref[:, base : base + width] = e
        start += width
    packed = lanes_to_rows(jnp.concatenate(tops, axis=1), rows).astype(jnp.bfloat16)
    plain_refs[0][:, widths[0] :] = packed
    for ref in keyed_refs:
        ref[:, base + widths[0] :] = packed


def weigh(high, low, orig, widths, value, cost):
    rows, states = value.shape
    base = high * cost.shape[2]
    outs = [((rows, w + (LANES if c == 0 else 0)), jnp.bfloat16) for c, w in enumerate(widths)]
    outs += [((rows, base + widths[0] + LANES), jnp.bfloat16)] * (low - 1)
    outs += [((rows, base), jnp.bfloat16)]
    kernel = functools.partial(weigh_kernel, high, low, orig, widths)
    return call(kernel, outs, 8 * rows * states, 8 * rows * states, (value, cost))


def sums_kernel(low, orig, chunk, widths, turns, open_ref, own_ref, *refs):
    groups = low * orig
    rows, base = own_ref.shape
    width = widths[chunk]
    first = sum(widths[:chunk]) // LANES
    skips = [base if b >= orig and b % orig == 0 else 0 for b in range(groups)]
    tops = [refs[b][:, skips[b] + widths[0] : skips[b] + widths[0] + LANES].astype(jnp.float32) for b in range(groups)]
    pieces = refs[:groups] if chunk == 0 else refs[groups : 2 * groups]
    out_refs = refs[-len(turns) :]
    for n, turn in enumerate(turns):
        feasible = [open_ref[turn * groups + b : turn * groups + b + 1, :] > 0.5 for b in range(groups)]
        ceiling = functools.reduce(jnp.maximum, [jnp.where(f, t, FLOOR) for f, t in zip(feasible, tops)])
        total = jnp.zeros((rows, width), jnp.float32)
        for i in range(low):
            key_ref = own_ref if i == 0 else refs[i * orig]
            for j in range(orig):
                b = i * orig + j
                scale = jnp.exp(jnp.where(feasible[b], tops[b] - ceiling, FLOOR))
                at = (turn * orig + j) * rows
                skip = skips[b] if chunk == 0 else 0
                product = jnp.dot(
                    key_ref[:, at : at + rows],
                    pieces[b][:, skip : skip + width],
                    preferred_element_type=jnp.float32,
                )
                total += rows_to_lanes(scale, first, width // LANES) * product
        out_refs[n][:, :width] = total.astype(jnp.bfloat16)
        if chunk == 0:
            out_refs[n][:, width:] = ceiling.astype(jnp.bfloat16)


def sums(low, orig, chunk, widths, turns, open_to, own_key, gathered):
    rows = own_key.shape[0]
    width = widths[chunk]
    groups = low * orig
    args = [open_to, own_key, *gathered[0]]
    if chunk > 0:
        args += gathered[chunk]
    outs = [((rows, width + (LANES if chunk == 0 else 0)), jnp.bfloat16)] * len(turns)
    kernel = functools.partial(sums_kernel, low, orig, chunk, widths, turns)
    flops = 2 * rows * rows * width * groups * len(turns)
    return call(kernel, outs, flops, 2 * rows * width * (groups + len(turns)), args)


def spot_kernel(high, low, orig, transition_ref, count_ref, list_ref, high_ref, onehot_ref, open_ref):
    nxt = transition_ref[pl.ds(lax.axis_index("st"), 1), :]
    high_ref[...] = lax.shift_right_logical(nxt, LOW_BITS)
    low_part = nxt & (onehot_ref.shape[0] - 1)
    rows = lax.broadcasted_iota(jnp.int32, onehot_ref.shape, 0)
    onehot_ref[...] = jnp.where(rows == low_part, 1.0, 0.0).astype(jnp.bfloat16)
    slots = list_ref.shape[1]
    my_high, my_low = place(low)
    my_orig = lax.axis_index("org")
    for turn in range(high):
        anchor = (((my_high + turn) % high) * low + my_low) * orig + my_orig
        limit = count_ref[anchor]
        for i in range(low):
            for j in range(orig):
                block = (my_high * low + (my_low + i) % low) * orig + (my_orig + j) % orig

                def hit(k, found):
                    return found | jnp.where((list_ref[anchor, k] == block) & (k < limit), 1, 0)

                found = lax.fori_loop(0, slots, hit, jnp.int32(0), unroll=slots <= 4)
                at = (turn * low + i) * orig + j
                open_ref[at : at + 1, :] = jnp.full((1, LANES), found.astype(jnp.float32))


def spot(high, low, orig, halves, transition, row_counts, dest_blocks):
    states = transition.shape[0] // halves
    size = 2**LOW_BITS
    outs = [
        ((1, states), jnp.int32),
        ((size, states), jnp.bfloat16),
        ((-(-high * low * orig // 8) * 8, LANES), jnp.float32),
    ]
    args = (transition.reshape(halves, states), row_counts, dest_blocks)
    kernel = functools.partial(spot_kernel, high, low, orig)
    return call(kernel, outs, 4 * size * states, 2 * size * states, args, smem=(1, 2))


def pick(halves, widths, chunks, where, onehot, states, got, value, ceiling):
    size = onehot.shape[0]
    rows = value.shape[0]
    per = size // LANES
    mine = lax.axis_index("st")
    stack, tops, parts = [], [], []
    for h in range(halves):
        part = ((mine + h) % halves) * (states // size)
        for chunk, ref in zip(chunks, got[h]):
            start = sum(widths[:chunk]) // size
            for k in range(widths[chunk] // size):
                stack.append(ref[:, k * size : (k + 1) * size])
                parts.append(part + start + k)
    every = jnp.dot(jnp.concatenate(stack, axis=0), onehot, preferred_element_type=jnp.float32)
    for n, part in enumerate(parts):
        value = jnp.where(where == part, every[n * rows : (n + 1) * rows, :], value)
    if chunks[0] == 0:
        for h in range(halves):
            c = got[h][0][:, widths[0] :].astype(jnp.float32)
            tops += [rows_to_lanes(c, k * per, per) for k in range(states // size)]
        every = jnp.dot(
            jnp.concatenate(tops, axis=0).astype(jnp.bfloat16), onehot, preferred_element_type=jnp.float32
        )
        for h in range(halves):
            part = ((mine + h) % halves) * (states // size)
            for k in range(states // size):
                n = h * (states // size) + k
                ceiling = jnp.where(where == part + k, every[n : n + 1, :], ceiling)
    return value, ceiling


def pick_kernel(halves, widths, chunks, where_ref, onehot_ref, *refs):
    value_ref, ceiling_ref = refs[-2:]
    got = [refs[h * len(chunks) : (h + 1) * len(chunks)] for h in range(halves)]
    rest = refs[halves * len(chunks) : -2]
    value = rest[0][...] if rest else jnp.zeros(value_ref.shape, jnp.float32)
    ceiling = rest[1][...] if rest else jnp.zeros(ceiling_ref.shape, jnp.float32)
    value_ref[...], ceiling_ref[...] = pick(
        halves, widths, chunks, where_ref[...], onehot_ref[...], where_ref.shape[1], got, value, ceiling
    )


def picked(halves, widths, chunks, marks, got, before=()):
    where, onehot = marks
    rows, states = got[0][0].shape[0], where.shape[1]
    outs = [((rows, states), jnp.float32), ((1, states), jnp.float32)]
    args = [where, onehot, *[x for per in got for x in per], *before]
    kernel = functools.partial(pick_kernel, halves, widths, chunks)
    width = sum(widths[c] for c in chunks)
    return call(kernel, outs, 2 * rows * states * width * halves, 4 * rows * states, args)


def finish_kernel(halves, widths, chunks, turns, tile, utility_ref, where_ref, onehot_ref, *refs):
    out_ref = refs[-1]
    here = pl.ds(pl.multiple_of(pl.program_id(0) * tile, tile), tile)
    count = halves * len(chunks)
    where, onehot = where_ref[:, here], onehot_ref[:, here]
    values, ceilings = [refs[0][:, here]], [refs[1][:, here]]
    refs = refs[2:-1]
    for _ in range(turns):
        got = [refs[h * len(chunks) : (h + 1) * len(chunks)] for h in range(halves)]
        refs = refs[count:]
        if chunks[0] > 0:
            value, ceiling = refs[0][:, here], refs[1][:, here]
            refs = refs[2:]
        else:
            value, ceiling = jnp.zeros(out_ref.shape, jnp.float32), jnp.zeros((1, tile), jnp.float32)
        value, ceiling = pick(halves, widths, chunks, where, onehot, where_ref.shape[1], got, value, ceiling)
        values.append(value)
        ceilings.append(ceiling)
    ceiling = functools.reduce(jnp.maximum, ceilings)
    merged = sum(v * jnp.exp(c - ceiling) for v, c in zip(values, ceilings))
    out_ref[...] = utility_ref[:, here] + DISCOUNT * (ceiling + jnp.log(merged))


def finish(halves, widths, chunks, utility, marks, own, others):
    rows, states = utility.shape
    tile = states // TILES
    args = [utility, *marks, *own]
    for got, before in others:
        args += [x for per in got for x in per]
        args += before
    kernel = functools.partial(finish_kernel, halves, widths, chunks, len(others), tile)
    flops = 2 * rows * states * states * halves
    return pl.pallas_call(
        kernel,
        grid=(TILES,),
        in_specs=[pl.BlockSpec(memory_space=pltpu.VMEM)] * len(args),
        out_specs=pl.BlockSpec((rows, tile), lambda n: (0, n)),
        out_shape=jax.ShapeDtypeStruct((rows, states), jnp.float32),
        compiler_params=pltpu.CompilerParams(vmem_limit_bytes=GRANT),
        cost_estimate=pl.CostEstimate(flops=flops, bytes_accessed=12 * rows * states, transcendentals=0),
        name="finish",
    )(*[pltpu.with_memory_space_constraint(a, pltpu.VMEM) for a in args])


def on_device(sizes, value_now, utility, move_costs, dest_blocks, row_counts, transition):
    dest, orig, halves = sizes
    low = 2 if dest % 2 == 0 else 1
    high = dest // low
    rows, states = value_now.shape[2:]
    widths = (states // CHUNKS,) * CHUNKS
    every = tuple(range(CHUNKS))
    both = ("dst", "org")

    def index(h, l, o):
        return (h * low + l) * orig + o

    def gather(x, i, j):
        pairs = [
            (index(h, l, o), index(h, (l - i) % low, (o - j) % orig))
            for h in range(high)
            for l in range(low)
            for o in range(orig)
        ]
        return lax.ppermute(x, both, pairs)

    def onward(x, r):
        pairs = [(h * low + l, ((h + r) % high) * low + l) for h in range(high) for l in range(low)]
        return lax.ppermute(x, "dst", pairs)

    def across(x):
        pairs = [[(s, (s - h) % halves) for s in range(halves)] for h in range(halves)]
        return [x if h == 0 else lax.ppermute(x, "st", pairs[h]) for h in range(halves)]

    def by_core(xs):
        return list(zip(*[across(x) for x in xs]))

    cost = move_costs.reshape(move_costs.shape[0], rows, move_costs.shape[4])
    made = weigh(high, low, orig, widths, value_now.reshape(rows, states), cost)
    plain, keyed, own_key = made[:CHUNKS], made[CHUNKS:-1], made[-1]
    gathered = []
    for c in every:
        row = []
        for i in range(low):
            for j in range(orig):
                x = keyed[i - 1] if c == 0 and i > 0 and j == 0 else plain[c]
                row.append(x if i == j == 0 else gather(x, i, j))
        gathered.append(row)
    *marks, open_to = spot(high, low, orig, halves, transition, row_counts, dest_blocks)
    step = functools.partial(sums, low, orig)
    rest = (open_to, own_key, gathered)
    turns = tuple(range(1, high))
    passed = []
    for c in every:
        sent = step(c, widths, turns, *rest) if turns else []
        passed.append([onward(x, r) for r, x in zip(turns, sent)])
    own = []
    for c in every:
        own += step(c, widths, (0,), *rest)
    own = by_core(own)
    own = picked(halves, widths, every, marks, own)
    others = []
    for n in range(len(turns)):
        before = ()
        for c in every[:-1]:
            got = by_core([passed[c][n]])
            before = picked(halves, widths, (c,), marks, got, before)
        others.append((by_core([passed[-1][n]]), before))
    out = finish(halves, widths, every[-1:], utility.reshape(rows, states), marks, own, others)
    return out.reshape(value_now.shape)


def solution(mesh):
    sizes = (mesh.shape["dst"], mesh.shape["org"], mesh.shape["st"])

    def body(*args):
        return on_device(sizes, *args)

    return jax.shard_map(
        body,
        mesh=mesh,
        in_specs=(
            P(("draws", "dst"), "org", None, "st"),
            P(("draws", "dst"), "org", None, "st"),
            P("draws", "org", None, "dst", None),
            P(),
            P(),
            P(),
        ),
        out_specs=P(("draws", "dst"), "org", None, "st"),
        check_vma=False,
    )
```

```python
import functools

import jax
import jax.numpy as jnp
from jax import lax
from jax.experimental import pallas as pl
from jax.experimental.pallas import tpu as pltpu
from jax.sharding import PartitionSpec as P


DISCOUNT = 0.95
FLOOR = -1e30
LANES = 128
CHUNKS = 2
LOW_BITS = 9
GRANT = 24 * 2**20
TILES = 2


def call(kernel, outs, flops, touched, args, smem=(), fetched=()):
    specs = [pl.BlockSpec(memory_space=pltpu.SMEM if n in smem else pltpu.VMEM) for n in range(len(args))]
    specs = [pl.BlockSpec() if n in fetched else spec for n, spec in enumerate(specs)]
    spaces = {n: pltpu.HBM for n in fetched}
    held = [
        a if n in smem else pltpu.with_memory_space_constraint(a, spaces.get(n, pltpu.VMEM)) for n, a in enumerate(args)
    ]
    return pl.pallas_call(
        kernel,
        in_specs=specs,
        out_specs=[pl.BlockSpec(memory_space=pltpu.VMEM)] * len(outs),
        out_shape=[pltpu.VMEM(shape, dtype) for shape, dtype in outs],
        compiler_params=pltpu.CompilerParams(vmem_limit_bytes=GRANT),
        cost_estimate=pl.CostEstimate(flops=flops, bytes_accessed=touched, transcendentals=0),
    )(*held)


def rows_to_lanes(block, first, count):
    return jnp.concatenate([block[first + i : first + i + 1, :] for i in range(count)], axis=1)


def lanes_to_rows(row, rows):
    count = row.shape[1] // LANES
    parts = [row[:, i * LANES : (i + 1) * LANES] for i in range(count)]
    if rows > count:
        parts.append(jnp.zeros((rows - count, LANES), row.dtype))
    return jnp.concatenate(parts, axis=0)


def place(low):
    d = lax.axis_index("dst")
    return d // low, d % low


def weigh_kernel(high, low, orig, widths, value_ref, cost_ref, *out_refs):
    plain_refs, keyed_refs, own_ref = out_refs[: len(widths)], out_refs[len(widths) : -1], out_refs[-1]
    my_high, my_low = place(low)
    my_orig = lax.axis_index("org")
    rows = value_ref.shape[0]
    cols = cost_ref.shape[2]

    def kernel_part(turn):
        target = (my_low + low - turn) % low
        parts = []
        for r in range(high):
            k = jnp.exp(-cost_ref[((my_high + r) % high) * low + target])
            turned = k
            for s in range(1, orig):
                turned = jnp.where(my_orig == s, pltpu.roll(k, cols - s * rows, 1), turned)
            parts.append(turned.astype(jnp.bfloat16))
        return parts

    for r, part in enumerate(kernel_part(0)):
        own_ref[:, r * cols : (r + 1) * cols] = part
    for turn in range(1, low):
        for r, part in enumerate(kernel_part(turn)):
            keyed_refs[turn - 1][:, r * cols : (r + 1) * cols] = part
    base = high * cols
    start = 0
    tops = []
    for c, width in enumerate(widths):
        v = value_ref[:, start : start + width]
        top = jnp.max(v, axis=0, keepdims=True).astype(jnp.bfloat16).astype(jnp.float32)
        tops.append(top)
        e = jnp.exp(v - top).astype(jnp.bfloat16)
        plain_refs[c][:, :width] = e
        if c == 0:
            for ref in keyed_refs:
                ref[:, base : base + width] = e
        start += width
    packed = lanes_to_rows(jnp.concatenate(tops, axis=1), rows).astype(jnp.bfloat16)
    plain_refs[0][:, widths[0] :] = packed
    for ref in keyed_refs:
        ref[:, base + widths[0] :] = packed


def weigh(high, low, orig, widths, value, cost):
    rows, states = value.shape
    base = high * cost.shape[2]
    outs = [((rows, w + (LANES if c == 0 else 0)), jnp.bfloat16) for c, w in enumerate(widths)]
    outs += [((rows, base + widths[0] + LANES), jnp.bfloat16)] * (low - 1)
    outs += [((rows, base), jnp.bfloat16)]
    kernel = functools.partial(weigh_kernel, high, low, orig, widths)
    return call(kernel, outs, 8 * rows * states, 8 * rows * states, (value, cost), fetched=(0, 1))


def sums_kernel(low, orig, chunk, widths, turns, open_ref, own_ref, *refs):
    groups = low * orig
    rows, base = own_ref.shape
    width = widths[chunk]
    first = sum(widths[:chunk]) // LANES
    skips = [base if b >= orig and b % orig == 0 else 0 for b in range(groups)]
    tops = [refs[b][:, skips[b] + widths[0] : skips[b] + widths[0] + LANES].astype(jnp.float32) for b in range(groups)]
    pieces = refs[:groups] if chunk == 0 else refs[groups : 2 * groups]
    out_refs = refs[-len(turns) :]
    for n, turn in enumerate(turns):
        feasible = [open_ref[turn * groups + b : turn * groups + b + 1, :] > 0.5 for b in range(groups)]
        ceiling = functools.reduce(jnp.maximum, [jnp.where(f, t, FLOOR) for f, t in zip(feasible, tops)])
        total = jnp.zeros((rows, width), jnp.float32)
        for i in range(low):
            key_ref = own_ref if i == 0 else refs[i * orig]
            for j in range(orig):
                b = i * orig + j
                scale = jnp.exp(jnp.where(feasible[b], tops[b] - ceiling, FLOOR))
                at = (turn * orig + j) * rows
                skip = skips[b] if chunk == 0 else 0
                product = jnp.dot(
                    key_ref[:, at : at + rows],
                    pieces[b][:, skip : skip + width],
                    preferred_element_type=jnp.float32,
                )
                total += rows_to_lanes(scale, first, width // LANES) * product
        out_refs[n][:, :width] = total.astype(jnp.bfloat16)
        if chunk == 0:
            out_refs[n][:, width:] = ceiling.astype(jnp.bfloat16)


def sums(low, orig, chunk, widths, turns, open_to, own_key, gathered):
    rows = own_key.shape[0]
    width = widths[chunk]
    groups = low * orig
    args = [open_to, own_key, *gathered[0]]
    if chunk > 0:
        args += gathered[chunk]
    outs = [((rows, width + (LANES if chunk == 0 else 0)), jnp.bfloat16)] * len(turns)
    kernel = functools.partial(sums_kernel, low, orig, chunk, widths, turns)
    flops = 2 * rows * rows * width * groups * len(turns)
    return call(kernel, outs, flops, 2 * rows * width * (groups + len(turns)), args)


def spot_kernel(high, low, orig, transition_ref, count_ref, list_ref, high_ref, onehot_ref, open_ref):
    nxt = transition_ref[pl.ds(lax.axis_index("st"), 1), :]
    high_ref[...] = lax.shift_right_logical(nxt, LOW_BITS)
    low_part = nxt & (onehot_ref.shape[0] - 1)
    rows = lax.broadcasted_iota(jnp.int32, onehot_ref.shape, 0)
    onehot_ref[...] = jnp.where(rows == low_part, 1.0, 0.0).astype(jnp.bfloat16)
    slots = list_ref.shape[1]
    my_high, my_low = place(low)
    my_orig = lax.axis_index("org")
    for turn in range(high):
        anchor = (((my_high + turn) % high) * low + my_low) * orig + my_orig
        limit = count_ref[anchor]
        for i in range(low):
            for j in range(orig):
                block = (my_high * low + (my_low + i) % low) * orig + (my_orig + j) % orig

                def hit(k, found):
                    return found | jnp.where((list_ref[anchor, k] == block) & (k < limit), 1, 0)

                found = lax.fori_loop(0, slots, hit, jnp.int32(0), unroll=slots <= 4)
                at = (turn * low + i) * orig + j
                open_ref[at : at + 1, :] = jnp.full((1, LANES), found.astype(jnp.float32))


def spot(high, low, orig, halves, transition, row_counts, dest_blocks):
    states = transition.shape[0] // halves
    size = 2**LOW_BITS
    outs = [
        ((1, states), jnp.int32),
        ((size, states), jnp.bfloat16),
        ((-(-high * low * orig // 8) * 8, LANES), jnp.float32),
    ]
    args = (transition.reshape(halves, states), row_counts, dest_blocks)
    kernel = functools.partial(spot_kernel, high, low, orig)
    return call(kernel, outs, 4 * size * states, 2 * size * states, args, smem=(1, 2))


def pick(halves, widths, chunks, where, onehot, states, got, value, ceiling):
    size = onehot.shape[0]
    rows = value.shape[0]
    per = size // LANES
    mine = lax.axis_index("st")
    stack, tops, parts = [], [], []
    for h in range(halves):
        part = ((mine + h) % halves) * (states // size)
        for chunk, ref in zip(chunks, got[h]):
            start = sum(widths[:chunk]) // size
            for k in range(widths[chunk] // size):
                stack.append(ref[:, k * size : (k + 1) * size])
                parts.append(part + start + k)
    every = jnp.dot(jnp.concatenate(stack, axis=0), onehot, preferred_element_type=jnp.float32)
    for n, part in enumerate(parts):
        value = jnp.where(where == part, every[n * rows : (n + 1) * rows, :], value)
    if chunks[0] == 0:
        for h in range(halves):
            c = got[h][0][:, widths[0] :].astype(jnp.float32)
            tops += [rows_to_lanes(c, k * per, per) for k in range(states // size)]
        every = jnp.dot(
            jnp.concatenate(tops, axis=0).astype(jnp.bfloat16), onehot, preferred_element_type=jnp.float32
        )
        for h in range(halves):
            part = ((mine + h) % halves) * (states // size)
            for k in range(states // size):
                n = h * (states // size) + k
                ceiling = jnp.where(where == part + k, every[n : n + 1, :], ceiling)
    return value, ceiling


def pick_kernel(halves, widths, chunks, where_ref, onehot_ref, *refs):
    value_ref, ceiling_ref = refs[-2:]
    got = [refs[h * len(chunks) : (h + 1) * len(chunks)] for h in range(halves)]
    rest = refs[halves * len(chunks) : -2]
    value = rest[0][...] if rest else jnp.zeros(value_ref.shape, jnp.float32)
    ceiling = rest[1][...] if rest else jnp.zeros(ceiling_ref.shape, jnp.float32)
    value_ref[...], ceiling_ref[...] = pick(
        halves, widths, chunks, where_ref[...], onehot_ref[...], where_ref.shape[1], got, value, ceiling
    )


def picked(halves, widths, chunks, marks, got, before=()):
    where, onehot = marks
    rows, states = got[0][0].shape[0], where.shape[1]
    outs = [((rows, states), jnp.float32), ((1, states), jnp.float32)]
    args = [where, onehot, *[x for per in got for x in per], *before]
    kernel = functools.partial(pick_kernel, halves, widths, chunks)
    width = sum(widths[c] for c in chunks)
    return call(kernel, outs, 2 * rows * states * width * halves, 4 * rows * states, args)


def finish_kernel(halves, widths, chunks, turns, tile, utility_ref, where_ref, onehot_ref, *refs):
    out_ref = refs[-1]
    here = pl.ds(pl.multiple_of(pl.program_id(0) * tile, tile), tile)
    count = halves * len(chunks)
    where, onehot = where_ref[:, here], onehot_ref[:, here]
    values, ceilings = [refs[0][:, here]], [refs[1][:, here]]
    refs = refs[2:-1]
    for _ in range(turns):
        got = [refs[h * len(chunks) : (h + 1) * len(chunks)] for h in range(halves)]
        refs = refs[count:]
        if chunks[0] > 0:
            value, ceiling = refs[0][:, here], refs[1][:, here]
            refs = refs[2:]
        else:
            value, ceiling = jnp.zeros(out_ref.shape, jnp.float32), jnp.zeros((1, tile), jnp.float32)
        value, ceiling = pick(halves, widths, chunks, where, onehot, where_ref.shape[1], got, value, ceiling)
        values.append(value)
        ceilings.append(ceiling)
    ceiling = functools.reduce(jnp.maximum, ceilings)
    merged = sum(v * jnp.exp(c - ceiling) for v, c in zip(values, ceilings))
    out_ref[...] = utility_ref[:, here] + DISCOUNT * (ceiling + jnp.log(merged))


def finish(halves, widths, chunks, utility, marks, own, others):
    rows, states = utility.shape
    tile = states // TILES
    args = [utility, *marks, *own]
    for got, before in others:
        args += [x for per in got for x in per]
        args += before
    kernel = functools.partial(finish_kernel, halves, widths, chunks, len(others), tile)
    flops = 2 * rows * states * states * halves
    return pl.pallas_call(
        kernel,
        grid=(TILES,),
        in_specs=[pl.BlockSpec(memory_space=pltpu.VMEM)] * len(args),
        out_specs=pl.BlockSpec((rows, tile), lambda n: (0, n)),
        out_shape=jax.ShapeDtypeStruct((rows, states), jnp.float32),
        compiler_params=pltpu.CompilerParams(vmem_limit_bytes=GRANT),
        cost_estimate=pl.CostEstimate(flops=flops, bytes_accessed=12 * rows * states, transcendentals=0),
        name="finish",
    )(*[pltpu.with_memory_space_constraint(a, pltpu.VMEM) for a in args])


def on_device(sizes, value_now, utility, move_costs, dest_blocks, row_counts, transition):
    dest, orig, halves = sizes
    low = 2 if dest % 2 == 0 else 1
    high = dest // low
    rows, states = value_now.shape[2:]
    pieces = states // 2**LOW_BITS
    widths = tuple((pieces + CHUNKS - 1 - c) // CHUNKS * 2**LOW_BITS for c in range(CHUNKS))
    every = tuple(range(CHUNKS))
    both = ("dst", "org")

    def index(h, l, o):
        return (h * low + l) * orig + o

    def gather(x, i, j):
        pairs = [
            (index(h, l, o), index(h, (l - i) % low, (o - j) % orig))
            for h in range(high)
            for l in range(low)
            for o in range(orig)
        ]
        return lax.ppermute(x, both, pairs)

    def onward(x, r):
        pairs = [(h * low + l, ((h + r) % high) * low + l) for h in range(high) for l in range(low)]
        return lax.ppermute(x, "dst", pairs)

    def across(x):
        pairs = [[(s, (s - h) % halves) for s in range(halves)] for h in range(halves)]
        return [x if h == 0 else lax.ppermute(x, "st", pairs[h]) for h in range(halves)]

    def by_core(xs):
        return list(zip(*[across(x) for x in xs]))

    cost = move_costs.reshape(move_costs.shape[0], rows, move_costs.shape[4])
    made = weigh(high, low, orig, widths, value_now.reshape(rows, states), cost)
    plain, keyed, own_key = made[:CHUNKS], made[CHUNKS:-1], made[-1]
    gathered = []
    for c in every:
        row = []
        for i in range(low):
            for j in range(orig):
                x = keyed[i - 1] if c == 0 and i > 0 and j == 0 else plain[c]
                row.append(x if i == j == 0 else gather(x, i, j))
        gathered.append(row)
    *marks, open_to = spot(high, low, orig, halves, transition, row_counts, dest_blocks)
    step = functools.partial(sums, low, orig)
    rest = (open_to, own_key, gathered)
    turns = tuple(range(1, high))
    passed = []
    for c in every:
        sent = step(c, widths, turns, *rest) if turns else []
        passed.append([onward(x, r) for r, x in zip(turns, sent)])
    own = []
    for c in every:
        own += step(c, widths, (0,), *rest)
    own = by_core(own)
    own = picked(halves, widths, every, marks, own)
    others = []
    for n in range(len(turns)):
        before = ()
        for c in every[:-1]:
            got = by_core([passed[c][n]])
            before = picked(halves, widths, (c,), marks, got, before)
        others.append((by_core([passed[-1][n]]), before))
    out = finish(halves, widths, every[-1:], utility.reshape(rows, states), marks, own, others)
    return out.reshape(value_now.shape)


def solution(mesh):
    sizes = (mesh.shape["dst"], mesh.shape["org"], mesh.shape["st"])

    def body(*args):
        return on_device(sizes, *args)

    return jax.shard_map(
        body,
        mesh=mesh,
        in_specs=(
            P(("draws", "dst"), "org", None, "st"),
            P(("draws", "dst"), "org", None, "st"),
            P("draws", "org", None, "dst", None),
            P(),
            P(),
            P(),
        ),
        out_specs=P(("draws", "dst"), "org", None, "st"),
        check_vma=False,
    )
```

```python
import functools

import jax
import jax.numpy as jnp
from jax import lax
from jax.experimental import pallas as pl
from jax.experimental.pallas import tpu as pltpu
from jax.sharding import PartitionSpec as P


DISCOUNT = 0.95
FLOOR = -1e30
LANES = 128
CHUNKS = 2
LOW_BITS = 8
GRANT = 24 * 2**20
TILES = 4


def call(kernel, outs, flops, touched, args, smem=(), fetched=()):
    specs = [pl.BlockSpec(memory_space=pltpu.SMEM if n in smem else pltpu.VMEM) for n in range(len(args))]
    specs = [pl.BlockSpec() if n in fetched else spec for n, spec in enumerate(specs)]
    spaces = {n: pltpu.HBM for n in fetched}
    held = [
        a if n in smem else pltpu.with_memory_space_constraint(a, spaces.get(n, pltpu.VMEM)) for n, a in enumerate(args)
    ]
    return pl.pallas_call(
        kernel,
        in_specs=specs,
        out_specs=[pl.BlockSpec(memory_space=pltpu.VMEM)] * len(outs),
        out_shape=[pltpu.VMEM(shape, dtype) for shape, dtype in outs],
        compiler_params=pltpu.CompilerParams(vmem_limit_bytes=GRANT),
        cost_estimate=pl.CostEstimate(flops=flops, bytes_accessed=touched, transcendentals=0),
    )(*held)


def put(ref, at, value):
    rows = value.shape[0]
    for n in range(value.shape[1] // LANES):
        ref[at + n * rows : at + (n + 1) * rows, :] = value[:, n * LANES : (n + 1) * LANES]
    return at + value.shape[1] // LANES * rows


def get(ref, at, rows, width):
    parts = [ref[at + n * rows : at + (n + 1) * rows, :] for n in range(width // LANES)]
    return jnp.concatenate(parts, axis=1)


def rows_to_lanes(block, first, count):
    return jnp.concatenate([block[first + i : first + i + 1, :] for i in range(count)], axis=1)


def lanes_to_rows(row):
    return jnp.concatenate([row[:, i : i + LANES] for i in range(0, row.shape[1], LANES)], axis=0)


def place(low):
    d = lax.axis_index("dst")
    return d // low, d % low


def weigh_kernel(high, low, orig, widths, value_ref, cost_ref, *out_refs):
    plain_refs, keyed_refs, own_ref = out_refs[: len(widths)], out_refs[len(widths) : -1], out_refs[-1]
    my_high, my_low = place(low)
    my_orig = lax.axis_index("org")
    rows = value_ref.shape[0]
    cols = cost_ref.shape[2]

    def kernel_part(turn):
        target = (my_low + low - turn) % low
        parts = []
        for r in range(high):
            k = jnp.exp(-cost_ref[((my_high + r) % high) * low + target])
            turned = k
            for s in range(1, orig):
                turned = jnp.where(my_orig == s, pltpu.roll(k, cols - s * rows, 1), turned)
            parts.append(turned.astype(jnp.bfloat16))
        return parts

    at = 0
    for part in kernel_part(0):
        at = put(own_ref, at, part)
    for turn in range(1, low):
        at = 0
        for part in kernel_part(turn):
            at = put(keyed_refs[turn - 1], at, part)
    start = 0
    tops = []
    for c, width in enumerate(widths):
        v = value_ref[:, start : start + width]
        top = jnp.max(v, axis=0, keepdims=True).astype(jnp.bfloat16).astype(jnp.float32)
        tops.append(top)
        e = jnp.exp(v - top).astype(jnp.bfloat16)
        end = put(plain_refs[c], 0, e)
        if c == 0:
            first = end
            for ref in keyed_refs:
                put(ref, own_ref.shape[0], e)
        start += width
    packed = lanes_to_rows(jnp.concatenate(tops, axis=1)).astype(jnp.bfloat16)
    plain_refs[0][first:, :] = packed
    for ref in keyed_refs:
        ref[own_ref.shape[0] + first :, :] = packed


def weigh(high, low, orig, widths, value, cost):
    rows, states = value.shape
    tops = states // LANES
    keys = high * rows * cost.shape[2] // LANES
    sizes = [rows * w // LANES + (tops if c == 0 else 0) for c, w in enumerate(widths)]
    sizes += [keys + sizes[0]] * (low - 1) + [keys]
    outs = [((size, LANES), jnp.bfloat16) for size in sizes]
    kernel = functools.partial(weigh_kernel, high, low, orig, widths)
    return call(kernel, outs, 8 * rows * states, 8 * rows * states, (value, cost), fetched=(0, 1))


def sums_kernel(low, orig, rows, chunk, widths, turns, open_ref, own_ref, *refs):
    groups = low * orig
    width = widths[chunk]
    first = sum(widths[:chunk]) // LANES
    keys = own_ref.shape[0]
    skips = [keys if b >= orig and b % orig == 0 else 0 for b in range(groups)]
    ends = [skip + rows * widths[0] // LANES for skip in skips]
    tops = [refs[b][ends[b] :, :].astype(jnp.float32) for b in range(groups)]
    pieces = refs[:groups] if chunk == 0 else refs[groups : 2 * groups]
    out_refs = refs[-len(turns) :]
    for n, turn in enumerate(turns):
        feasible = [open_ref[turn * groups + b : turn * groups + b + 1, :] > 0.5 for b in range(groups)]
        ceiling = functools.reduce(jnp.maximum, [jnp.where(f, t, FLOOR) for f, t in zip(feasible, tops)])
        total = jnp.zeros((rows, width), jnp.float32)
        for i in range(low):
            key_ref = own_ref if i == 0 else refs[i * orig]
            for j in range(orig):
                b = i * orig + j
                scale = jnp.exp(jnp.where(feasible[b], tops[b] - ceiling, FLOOR))
                column = (turn * orig + j) * rows
                at, column = column // LANES * rows, column % LANES
                product = jnp.dot(
                    key_ref[at : at + rows, column : column + rows],
                    get(pieces[b], skips[b] if chunk == 0 else 0, rows, width),
                    preferred_element_type=jnp.float32,
                )
                total += rows_to_lanes(scale, first, width // LANES) * product
        end = put(out_refs[n], 0, total.astype(jnp.bfloat16))
        if chunk == 0:
            out_refs[n][end:, :] = ceiling.astype(jnp.bfloat16)


def sums(low, orig, rows, chunk, widths, turns, open_to, own_key, gathered):
    width = widths[chunk]
    groups = low * orig
    args = [open_to, own_key, *gathered[0]]
    if chunk > 0:
        args += gathered[chunk]
    size = rows * width // LANES + (sum(widths) // LANES if chunk == 0 else 0)
    outs = [((size, LANES), jnp.bfloat16)] * len(turns)
    kernel = functools.partial(sums_kernel, low, orig, rows, chunk, widths, turns)
    flops = 2 * rows * rows * width * groups * len(turns)
    return call(kernel, outs, flops, 2 * rows * width * (groups + len(turns)), args)


def spot_kernel(high, low, orig, transition_ref, count_ref, list_ref, high_ref, onehot_ref, open_ref):
    nxt = transition_ref[pl.ds(lax.axis_index("st"), 1), :]
    high_ref[...] = lax.shift_right_logical(nxt, LOW_BITS)
    low_part = nxt & (onehot_ref.shape[0] - 1)
    rows = lax.broadcasted_iota(jnp.int32, onehot_ref.shape, 0)
    onehot_ref[...] = jnp.where(rows == low_part, 1.0, 0.0).astype(jnp.bfloat16)
    slots = list_ref.shape[1]
    my_high, my_low = place(low)
    my_orig = lax.axis_index("org")
    for turn in range(high):
        anchor = (((my_high + turn) % high) * low + my_low) * orig + my_orig
        limit = count_ref[anchor]
        for i in range(low):
            for j in range(orig):
                block = (my_high * low + (my_low + i) % low) * orig + (my_orig + j) % orig

                def hit(k, found):
                    return found | jnp.where((list_ref[anchor, k] == block) & (k < limit), 1, 0)

                found = lax.fori_loop(0, slots, hit, jnp.int32(0), unroll=slots <= 4)
                at = (turn * low + i) * orig + j
                open_ref[at : at + 1, :] = jnp.full((1, LANES), found.astype(jnp.float32))


def spot(high, low, orig, halves, transition, row_counts, dest_blocks):
    states = transition.shape[0] // halves
    size = 2**LOW_BITS
    outs = [
        ((1, states), jnp.int32),
        ((size, states), jnp.bfloat16),
        ((-(-high * low * orig // 8) * 8, LANES), jnp.float32),
    ]
    args = (transition.reshape(halves, states), row_counts, dest_blocks)
    kernel = functools.partial(spot_kernel, high, low, orig)
    return call(kernel, outs, 4 * size * states, 2 * size * states, args, smem=(1, 2))


def pick(halves, cores, widths, chunk, where, onehot, states, got, value):
    size = onehot.shape[0]
    rows = value.shape[0]
    mine = lax.axis_index("st")
    start = sum(widths[:chunk]) // size
    stack, parts = [], []
    for h, ref in zip(cores, got):
        part = ((mine + h) % halves) * (states // size) + start
        for k in range(widths[chunk] // size):
            stack.append(get(ref, k * size // LANES * rows, rows, size))
            parts.append(part + k)
    every = jnp.dot(jnp.concatenate(stack, axis=0), onehot, preferred_element_type=jnp.float32)
    for n, part in enumerate(parts):
        value = jnp.where(where == part, every[n * rows : (n + 1) * rows, :], value)
    return value


def pick_ceiling(halves, rows, widths, where, onehot, states, got):
    size = onehot.shape[0]
    mine = lax.axis_index("st")
    per = size // LANES
    tops, parts = [], []
    for h in range(halves):
        c = got[h][rows * widths[0] // LANES :, :].astype(jnp.float32)
        for k in range(states // size):
            tops.append(rows_to_lanes(c, k * per, per))
            parts.append(((mine + h) % halves) * (states // size) + k)
    every = jnp.dot(
        jnp.concatenate(tops, axis=0).astype(jnp.bfloat16), onehot, preferred_element_type=jnp.float32
    )
    ceiling = jnp.zeros(where.shape, jnp.float32)
    for n, part in enumerate(parts):
        ceiling = jnp.where(where == part, every[n : n + 1, :], ceiling)
    return ceiling


def pick_kernel(halves, widths, chunks, where_ref, onehot_ref, *refs):
    value_ref, ceiling_ref = refs[-2:]
    got = [refs[n * halves : (n + 1) * halves] for n in range(len(chunks))]
    rest = refs[halves * len(chunks) : -2]
    where, onehot, states = where_ref[...], onehot_ref[...], where_ref.shape[1]
    value = rest[0][...] if rest else jnp.zeros(value_ref.shape, jnp.float32)
    for chunk, per_core in zip(chunks, got):
        value = pick(halves, range(halves), widths, chunk, where, onehot, states, per_core, value)
    value_ref[...] = value
    if chunks[0] == 0:
        ceiling_ref[...] = pick_ceiling(halves, value.shape[0], widths, where, onehot, states, got[0])
    else:
        ceiling_ref[...] = rest[1][...]


def picked(halves, rows, widths, chunks, marks, got, before=()):
    where, onehot = marks
    states = where.shape[1]
    outs = [((rows, states), jnp.float32), ((1, states), jnp.float32)]
    args = [where, onehot, *[x for per_core in got for x in per_core], *before]
    kernel = functools.partial(pick_kernel, halves, widths, chunks)
    width = sum(widths[c] for c in chunks)
    return call(kernel, outs, 2 * rows * states * width * halves, 4 * rows * states, args)


def settle_kernel(halves, widths, turns, utility_ref, where_ref, onehot_ref, own_ref, top_ref, *refs):
    known_ref, base_ref = refs[3 * turns : 3 * turns + 2]
    scale_refs = refs[3 * turns + 2 :]
    where, onehot, states = where_ref[...], onehot_ref[...], where_ref.shape[1]
    tops = [top_ref[...]] + [refs[3 * n + 2][...] for n in range(turns)]
    ceiling = functools.reduce(jnp.maximum, tops)
    known = own_ref[...] * jnp.exp(tops[0] - ceiling)
    for n in range(turns):
        scale = jnp.exp(tops[n + 1] - ceiling)
        value = pick(halves, (0,), widths, len(widths) - 1, where, onehot, states, refs[3 * n : 3 * n + 1], refs[3 * n + 1][...])
        known += scale * value
        scale_refs[n][...] = scale
    known_ref[...] = known
    base_ref[...] = utility_ref[...] + DISCOUNT * ceiling


def settle(halves, widths, utility, marks, own, others):
    rows, states = utility.shape
    args = [utility, *marks, *own]
    for got, before in others:
        args += [got, *before]
    outs = [((rows, states), jnp.float32)] * 2 + [((1, states), jnp.float32)] * len(others)
    kernel = functools.partial(settle_kernel, halves, widths, len(others))
    flops = 2 * rows * states * widths[-1] * len(others)
    return call(kernel, outs, flops, 16 * rows * states, args)


def finish_kernel(halves, widths, turns, tile, where_ref, onehot_ref, known_ref, base_ref, *refs):
    *refs, out_ref, held_ref, sems = refs
    rows, states = known_ref.shape
    copies = []
    for start in range(0, states, tile):
        here = slice(start, start + tile)
        where, onehot = where_ref[:, here], onehot_ref[:, here]
        merged = known_ref[:, here]
        for n in range(turns):
            got = refs[turns + n * (halves - 1) : turns + (n + 1) * (halves - 1)]
            zero = jnp.zeros((rows, tile), jnp.float32)
            value = pick(halves, range(1, halves), widths, len(widths) - 1, where, onehot, states, got, zero)
            merged += refs[n][:, here] * value
        held_ref[:, here] = base_ref[:, here] + DISCOUNT * jnp.log(merged)
        copy = pltpu.make_async_copy(held_ref.at[:, here], out_ref.at[:, here], sems.at[start // tile])
        copy.start()
        copies.append(copy)
    for copy in copies:
        copy.wait()


def finish(halves, widths, marks, settled, others):
    known, base, *scales = settled
    rows, states = known.shape
    args = [*marks, known, base, *scales, *[x for got in others for x in got]]
    kernel = functools.partial(finish_kernel, halves, widths, len(others), states // TILES)
    flops = 2 * rows * states * widths[-1] * (halves - 1) * len(others)
    return pl.pallas_call(
        kernel,
        in_specs=[pl.BlockSpec(memory_space=pltpu.VMEM)] * len(args),
        out_specs=pl.BlockSpec(memory_space=pltpu.HBM),
        out_shape=pltpu.HBM((rows, states), jnp.float32),
        scratch_shapes=[pltpu.VMEM((rows, states), jnp.float32), pltpu.SemaphoreType.DMA((TILES,))],
        compiler_params=pltpu.CompilerParams(vmem_limit_bytes=GRANT),
        cost_estimate=pl.CostEstimate(flops=flops, bytes_accessed=12 * rows * states, transcendentals=0),
        name="finish",
    )(*[pltpu.with_memory_space_constraint(a, pltpu.VMEM) for a in args])


def on_device(sizes, value_now, utility, move_costs, dest_blocks, row_counts, transition):
    dest, orig, halves = sizes
    low = 2 if dest % 2 == 0 else 1
    high = dest // low
    rows, states = value_now.shape[2:]
    pieces = states // 2**LOW_BITS
    widths = tuple((pieces + CHUNKS - 1 - c) // CHUNKS * 2**LOW_BITS for c in range(CHUNKS))
    every = tuple(range(CHUNKS))
    both = ("dst", "org")

    def index(h, l, o):
        return (h * low + l) * orig + o

    def gather(x, i, j):
        pairs = [
            (index(h, l, o), index(h, (l - i) % low, (o - j) % orig))
            for h in range(high)
            for l in range(low)
            for o in range(orig)
        ]
        return lax.ppermute(x, both, pairs)

    def onward(x, r):
        pairs = [(h * low + l, ((h + r) % high) * low + l) for h in range(high) for l in range(low)]
        return lax.ppermute(x, "dst", pairs)

    def across(x):
        pairs = [[(s, (s - h) % halves) for s in range(halves)] for h in range(halves)]
        return [x if h == 0 else lax.ppermute(x, "st", pairs[h]) for h in range(halves)]

    cost = move_costs.reshape(move_costs.shape[0], rows, move_costs.shape[4])
    made = weigh(high, low, orig, widths, value_now.reshape(rows, states), cost)
    plain, keyed, own_key = made[:CHUNKS], made[CHUNKS:-1], made[-1]
    gathered = []
    for c in every:
        row = []
        for i in range(low):
            for j in range(orig):
                x = keyed[i - 1] if c == 0 and i > 0 and j == 0 else plain[c]
                row.append(x if i == j == 0 else gather(x, i, j))
        gathered.append(row)
    *marks, open_to = spot(high, low, orig, halves, transition, row_counts, dest_blocks)
    step = functools.partial(sums, low, orig, rows)
    rest = (open_to, own_key, gathered)
    turns = tuple(range(1, high))
    passed = []
    for c in every:
        sent = step(c, widths, turns, *rest) if turns else []
        passed.append([onward(x, r) for r, x in zip(turns, sent)])
    own = []
    for c in every:
        own += step(c, widths, (0,), *rest)
    own = [across(x) for x in own]
    own = picked(halves, rows, widths, every, marks, own)
    near, far = [], []
    for n in range(len(turns)):
        before = ()
        for c in every[:-1]:
            got = across(passed[c][n])
            before = picked(halves, rows, widths, (c,), marks, [got], before)
        here, *there = across(passed[-1][n])
        near.append((here, before))
        far.append(there)
    settled = settle(halves, widths, utility.reshape(rows, states), marks, own, near)
    out = finish(halves, widths, marks, settled, far)
    return out.reshape(value_now.shape)


def solution(mesh):
    sizes = (mesh.shape["dst"], mesh.shape["org"], mesh.shape["st"])

    def body(*args):
        return on_device(sizes, *args)

    return jax.shard_map(
        body,
        mesh=mesh,
        in_specs=(
            P(("draws", "dst"), "org", None, "st"),
            P(("draws", "dst"), "org", None, "st"),
            P("draws", "org", None, "dst", None),
            P(),
            P(),
            P(),
        ),
        out_specs=P(("draws", "dst"), "org", None, "st"),
        check_vma=False,
    )
```

```python
import functools

import jax
import jax.numpy as jnp
from jax import lax
from jax.experimental import pallas as pl
from jax.experimental.pallas import tpu as pltpu
from jax.sharding import PartitionSpec as P


DISCOUNT = 0.95
FLOOR = -1e30
LANES = 128
CHUNKS = 2
LOW_BITS = 8
GRANT = 24 * 2**20
TILES = 4


def call(kernel, outs, flops, touched, args, smem=(), fetched=()):
    specs = [pl.BlockSpec(memory_space=pltpu.SMEM if n in smem else pltpu.VMEM) for n in range(len(args))]
    specs = [pl.BlockSpec() if n in fetched else spec for n, spec in enumerate(specs)]
    spaces = {n: pltpu.HBM for n in fetched}
    held = [
        a if n in smem else pltpu.with_memory_space_constraint(a, spaces.get(n, pltpu.VMEM)) for n, a in enumerate(args)
    ]
    return pl.pallas_call(
        kernel,
        in_specs=specs,
        out_specs=[pl.BlockSpec(memory_space=pltpu.VMEM)] * len(outs),
        out_shape=[pltpu.VMEM(shape, dtype) for shape, dtype in outs],
        compiler_params=pltpu.CompilerParams(vmem_limit_bytes=GRANT),
        cost_estimate=pl.CostEstimate(flops=flops, bytes_accessed=touched, transcendentals=0),
    )(*held)


def put(ref, at, value):
    rows = value.shape[0]
    for n in range(value.shape[1] // LANES):
        ref[at + n * rows : at + (n + 1) * rows, :] = value[:, n * LANES : (n + 1) * LANES]
    return at + value.shape[1] // LANES * rows


def get(ref, at, rows, width):
    parts = [ref[at + n * rows : at + (n + 1) * rows, :] for n in range(width // LANES)]
    return jnp.concatenate(parts, axis=1)


def rows_to_lanes(block, first, count):
    return jnp.concatenate([block[first + i : first + i + 1, :] for i in range(count)], axis=1)


def lanes_to_rows(row):
    return jnp.concatenate([row[:, i : i + LANES] for i in range(0, row.shape[1], LANES)], axis=0)


def place(low):
    d = lax.axis_index("dst")
    return d // low, d % low


def weigh_kernel(high, low, orig, widths, value_ref, cost_ref, *out_refs):
    plain_refs, own_ref = out_refs[: len(widths)], out_refs[-1]
    keyed_refs, late_refs = out_refs[len(widths) : len(widths) + low - 1], out_refs[len(widths) + low - 1 : -1]
    base = own_ref.shape[0] // high * (high - 1)
    my_high, my_low = place(low)
    my_orig = lax.axis_index("org")
    rows = value_ref.shape[0]
    cols = cost_ref.shape[2]

    def kernel_part(turn):
        target = (my_low + low - turn) % low
        parts = []
        for r in range(high):
            k = jnp.exp(-cost_ref[((my_high + r) % high) * low + target])
            turned = k
            for s in range(1, orig):
                turned = jnp.where(my_orig == s, pltpu.roll(k, cols - s * rows, 1), turned)
            parts.append(turned.astype(jnp.bfloat16))
        return parts

    at = 0
    for part in kernel_part(0):
        at = put(own_ref, at, part)
    for turn in range(1, low):
        at = 0
        late, *parts = kernel_part(turn)
        put(late_refs[turn - 1], 0, late)
        for part in parts:
            at = put(keyed_refs[turn - 1], at, part)
    start = 0
    tops = []
    for c, width in enumerate(widths):
        v = value_ref[:, start : start + width]
        top = jnp.max(v, axis=0, keepdims=True).astype(jnp.bfloat16).astype(jnp.float32)
        tops.append(top)
        e = jnp.exp(v - top).astype(jnp.bfloat16)
        end = put(plain_refs[c], 0, e)
        if c == 0:
            first = end
            for ref in keyed_refs:
                put(ref, base, e)
        start += width
    packed = lanes_to_rows(jnp.concatenate(tops, axis=1)).astype(jnp.bfloat16)
    plain_refs[0][first:, :] = packed
    for ref in keyed_refs:
        ref[base + first :, :] = packed


def weigh(high, low, orig, widths, value, cost):
    rows, states = value.shape
    tops = states // LANES
    keys = high * rows * cost.shape[2] // LANES
    sizes = [rows * w // LANES + (tops if c == 0 else 0) for c, w in enumerate(widths)]
    sizes += [keys // high * (high - 1) + sizes[0]] * (low - 1) + [keys // high] * (low - 1) + [keys]
    outs = [((size, LANES), jnp.bfloat16) for size in sizes]
    kernel = functools.partial(weigh_kernel, high, low, orig, widths)
    return call(kernel, outs, 8 * rows * states, 8 * rows * states, (value, cost), fetched=(0, 1))


def sums_kernel(high, low, orig, rows, chunk, widths, turns, open_ref, own_ref, *refs):
    groups = low * orig
    width = widths[chunk]
    first = sum(widths[:chunk]) // LANES
    keys = own_ref.shape[0] // high * (high - 1)
    late = low - 1 if 0 in turns else 0
    late_refs, refs = refs[:late], refs[late:]
    skips = [keys if b >= orig and b % orig == 0 else 0 for b in range(groups)]
    ends = [skip + rows * widths[0] // LANES for skip in skips]
    tops = [refs[b][ends[b] :, :].astype(jnp.float32) for b in range(groups)]
    pieces = refs[:groups] if chunk == 0 else refs[groups : 2 * groups]
    out_refs = refs[-len(turns) :]
    for n, turn in enumerate(turns):
        feasible = [open_ref[turn * groups + b : turn * groups + b + 1, :] > 0.5 for b in range(groups)]
        ceiling = functools.reduce(jnp.maximum, [jnp.where(f, t, FLOOR) for f, t in zip(feasible, tops)])
        total = jnp.zeros((rows, width), jnp.float32)
        for i in range(low):
            key_ref, nth = own_ref, turn
            if i > 0:
                key_ref, nth = (late_refs[i - 1], 0) if turn == 0 else (refs[i * orig], turn - 1)
            for j in range(orig):
                b = i * orig + j
                scale = jnp.exp(jnp.where(feasible[b], tops[b] - ceiling, FLOOR))
                column = (nth * orig + j) * rows
                at, column = column // LANES * rows, column % LANES
                product = jnp.dot(
                    key_ref[at : at + rows, column : column + rows],
                    get(pieces[b], skips[b] if chunk == 0 else 0, rows, width),
                    preferred_element_type=jnp.float32,
                )
                total += rows_to_lanes(scale, first, width // LANES) * product
        end = put(out_refs[n], 0, total.astype(jnp.bfloat16))
        if chunk == 0:
            out_refs[n][end:, :] = ceiling.astype(jnp.bfloat16)


def sums(high, low, orig, rows, chunk, widths, turns, open_to, own_key, late, gathered):
    width = widths[chunk]
    groups = low * orig
    args = [open_to, own_key, *(late if 0 in turns else ()), *gathered[0]]
    if chunk > 0:
        args += gathered[chunk]
    size = rows * width // LANES + (sum(widths) // LANES if chunk == 0 else 0)
    outs = [((size, LANES), jnp.bfloat16)] * len(turns)
    kernel = functools.partial(sums_kernel, high, low, orig, rows, chunk, widths, turns)
    flops = 2 * rows * rows * width * groups * len(turns)
    return call(kernel, outs, flops, 2 * rows * width * (groups + len(turns)), args)


def spot_kernel(high, low, orig, transition_ref, count_ref, list_ref, high_ref, onehot_ref, open_ref):
    nxt = transition_ref[pl.ds(lax.axis_index("st"), 1), :]
    high_ref[...] = lax.shift_right_logical(nxt, LOW_BITS)
    low_part = nxt & (onehot_ref.shape[0] - 1)
    rows = lax.broadcasted_iota(jnp.int32, onehot_ref.shape, 0)
    onehot_ref[...] = jnp.where(rows == low_part, 1.0, 0.0).astype(jnp.bfloat16)
    slots = list_ref.shape[1]
    my_high, my_low = place(low)
    my_orig = lax.axis_index("org")
    for turn in range(high):
        anchor = (((my_high + turn) % high) * low + my_low) * orig + my_orig
        limit = count_ref[anchor]
        for i in range(low):
            for j in range(orig):
                block = (my_high * low + (my_low + i) % low) * orig + (my_orig + j) % orig

                def hit(k, found):
                    return found | jnp.where((list_ref[anchor, k] == block) & (k < limit), 1, 0)

                found = lax.fori_loop(0, slots, hit, jnp.int32(0), unroll=slots <= 4)
                at = (turn * low + i) * orig + j
                open_ref[at : at + 1, :] = jnp.full((1, LANES), found.astype(jnp.float32))


def spot(high, low, orig, halves, transition, row_counts, dest_blocks):
    states = transition.shape[0] // halves
    size = 2**LOW_BITS
    outs = [
        ((1, states), jnp.int32),
        ((size, states), jnp.bfloat16),
        ((-(-high * low * orig // 8) * 8, LANES), jnp.float32),
    ]
    args = (transition.reshape(halves, states), row_counts, dest_blocks)
    kernel = functools.partial(spot_kernel, high, low, orig)
    return call(kernel, outs, 4 * size * states, 2 * size * states, args, smem=(1, 2))


def pick(halves, cores, widths, chunk, where, onehot, states, got, value):
    size = onehot.shape[0]
    rows = value.shape[0]
    mine = lax.axis_index("st")
    start = sum(widths[:chunk]) // size
    stack, parts = [], []
    for h, ref in zip(cores, got):
        part = ((mine + h) % halves) * (states // size) + start
        for k in range(widths[chunk] // size):
            stack.append(get(ref, k * size // LANES * rows, rows, size))
            parts.append(part + k)
    every = jnp.dot(jnp.concatenate(stack, axis=0), onehot, preferred_element_type=jnp.float32)
    for n, part in enumerate(parts):
        value = jnp.where(where == part, every[n * rows : (n + 1) * rows, :], value)
    return value


def pick_ceiling(halves, rows, widths, where, onehot, states, got):
    size = onehot.shape[0]
    mine = lax.axis_index("st")
    per = size // LANES
    tops, parts = [], []
    for h in range(halves):
        c = got[h][rows * widths[0] // LANES :, :].astype(jnp.float32)
        for k in range(states // size):
            tops.append(rows_to_lanes(c, k * per, per))
            parts.append(((mine + h) % halves) * (states // size) + k)
    every = jnp.dot(
        jnp.concatenate(tops, axis=0).astype(jnp.bfloat16), onehot, preferred_element_type=jnp.float32
    )
    ceiling = jnp.zeros(where.shape, jnp.float32)
    for n, part in enumerate(parts):
        ceiling = jnp.where(where == part, every[n : n + 1, :], ceiling)
    return ceiling


def pick_kernel(halves, widths, chunks, where_ref, onehot_ref, *refs):
    value_ref, ceiling_ref = refs[-2:]
    got = [refs[n * halves : (n + 1) * halves] for n in range(len(chunks))]
    rest = refs[halves * len(chunks) : -2]
    where, onehot, states = where_ref[...], onehot_ref[...], where_ref.shape[1]
    value = rest[0][...] if rest else jnp.zeros(value_ref.shape, jnp.float32)
    for chunk, per_core in zip(chunks, got):
        value = pick(halves, range(halves), widths, chunk, where, onehot, states, per_core, value)
    value_ref[...] = value
    if chunks[0] == 0:
        ceiling_ref[...] = pick_ceiling(halves, value.shape[0], widths, where, onehot, states, got[0])
    else:
        ceiling_ref[...] = rest[1][...]


def picked(halves, rows, widths, chunks, marks, got, before=()):
    where, onehot = marks
    states = where.shape[1]
    outs = [((rows, states), jnp.float32), ((1, states), jnp.float32)]
    args = [where, onehot, *[x for per_core in got for x in per_core], *before]
    kernel = functools.partial(pick_kernel, halves, widths, chunks)
    width = sum(widths[c] for c in chunks)
    return call(kernel, outs, 2 * rows * states * width * halves, 4 * rows * states, args)


def settle_kernel(halves, widths, turns, utility_ref, where_ref, onehot_ref, own_ref, top_ref, *refs):
    known_ref, base_ref = refs[3 * turns : 3 * turns + 2]
    scale_refs = refs[3 * turns + 2 :]
    where, onehot, states = where_ref[...], onehot_ref[...], where_ref.shape[1]
    tops = [top_ref[...]] + [refs[3 * n + 2][...] for n in range(turns)]
    ceiling = functools.reduce(jnp.maximum, tops)
    known = own_ref[...] * jnp.exp(tops[0] - ceiling)
    for n in range(turns):
        scale = jnp.exp(tops[n + 1] - ceiling)
        value = pick(halves, (0,), widths, len(widths) - 1, where, onehot, states, refs[3 * n : 3 * n + 1], refs[3 * n + 1][...])
        known += scale * value
        scale_refs[n][...] = scale
    known_ref[...] = known
    base_ref[...] = utility_ref[...] + DISCOUNT * ceiling


def settle(halves, widths, utility, marks, own, others):
    rows, states = utility.shape
    args = [utility, *marks, *own]
    for got, before in others:
        args += [got, *before]
    outs = [((rows, states), jnp.float32)] * 2 + [((1, states), jnp.float32)] * len(others)
    kernel = functools.partial(settle_kernel, halves, widths, len(others))
    flops = 2 * rows * states * widths[-1] * len(others)
    return call(kernel, outs, flops, 16 * rows * states, args)


def finish_kernel(halves, widths, turns, tile, where_ref, onehot_ref, known_ref, base_ref, *refs):
    *refs, out_ref, held_ref, sems = refs
    rows, states = known_ref.shape
    copies = []
    for start in range(0, states, tile):
        here = slice(start, start + tile)
        where, onehot = where_ref[:, here], onehot_ref[:, here]
        merged = known_ref[:, here]
        for n in range(turns):
            got = refs[turns + n * (halves - 1) : turns + (n + 1) * (halves - 1)]
            zero = jnp.zeros((rows, tile), jnp.float32)
            value = pick(halves, range(1, halves), widths, len(widths) - 1, where, onehot, states, got, zero)
            merged += refs[n][:, here] * value
        held_ref[:, here] = base_ref[:, here] + DISCOUNT * jnp.log(merged)
        copy = pltpu.make_async_copy(held_ref.at[:, here], out_ref.at[:, here], sems.at[start // tile])
        copy.start()
        copies.append(copy)
    for copy in copies:
        copy.wait()


def finish(halves, widths, marks, settled, others):
    known, base, *scales = settled
    rows, states = known.shape
    args = [*marks, known, base, *scales, *[x for got in others for x in got]]
    kernel = functools.partial(finish_kernel, halves, widths, len(others), states // TILES)
    flops = 2 * rows * states * widths[-1] * (halves - 1) * len(others)
    return pl.pallas_call(
        kernel,
        in_specs=[pl.BlockSpec(memory_space=pltpu.VMEM)] * len(args),
        out_specs=pl.BlockSpec(memory_space=pltpu.HBM),
        out_shape=pltpu.HBM((rows, states), jnp.float32),
        scratch_shapes=[pltpu.VMEM((rows, states), jnp.float32), pltpu.SemaphoreType.DMA((TILES,))],
        compiler_params=pltpu.CompilerParams(vmem_limit_bytes=GRANT),
        cost_estimate=pl.CostEstimate(flops=flops, bytes_accessed=12 * rows * states, transcendentals=0),
        name="finish",
    )(*[pltpu.with_memory_space_constraint(a, pltpu.VMEM) for a in args])


def on_device(sizes, value_now, utility, move_costs, dest_blocks, row_counts, transition):
    dest, orig, halves = sizes
    low = 2 if dest % 2 == 0 else 1
    high = dest // low
    rows, states = value_now.shape[2:]
    pieces = states // 2**LOW_BITS
    widths = tuple((pieces + CHUNKS - 1 - c) // CHUNKS * 2**LOW_BITS for c in range(CHUNKS))
    every = tuple(range(CHUNKS))
    both = ("dst", "org")

    def index(h, l, o):
        return (h * low + l) * orig + o

    def gather(x, i, j):
        pairs = [
            (index(h, l, o), index(h, (l - i) % low, (o - j) % orig))
            for h in range(high)
            for l in range(low)
            for o in range(orig)
        ]
        return lax.ppermute(x, both, pairs)

    def onward(x, r):
        pairs = [(h * low + l, ((h + r) % high) * low + l) for h in range(high) for l in range(low)]
        return lax.ppermute(x, "dst", pairs)

    def across(x):
        pairs = [[(s, (s - h) % halves) for s in range(halves)] for h in range(halves)]
        return [x if h == 0 else lax.ppermute(x, "st", pairs[h]) for h in range(halves)]

    cost = move_costs.reshape(move_costs.shape[0], rows, move_costs.shape[4])
    made = weigh(high, low, orig, widths, value_now.reshape(rows, states), cost)
    plain, own_key = made[:CHUNKS], made[-1]
    keyed, late = made[CHUNKS : CHUNKS + low - 1], made[CHUNKS + low - 1 : -1]
    late = [gather(x, i, 0) for i, x in enumerate(late, 1)]
    gathered = []
    for c in every:
        row = []
        for i in range(low):
            for j in range(orig):
                x = keyed[i - 1] if c == 0 and i > 0 and j == 0 else plain[c]
                row.append(x if i == j == 0 else gather(x, i, j))
        gathered.append(row)
    *marks, open_to = spot(high, low, orig, halves, transition, row_counts, dest_blocks)
    step = functools.partial(sums, high, low, orig, rows)
    rest = (open_to, own_key, late, gathered)
    turns = tuple(range(1, high))
    passed = []
    for c in every:
        sent = step(c, widths, turns, *rest) if turns else []
        passed.append([onward(x, r) for r, x in zip(turns, sent)])
    own = []
    for c in every:
        own += step(c, widths, (0,), *rest)
    own = [across(x) for x in own]
    own = picked(halves, rows, widths, every, marks, own)
    near, far = [], []
    for n in range(len(turns)):
        before = ()
        for c in every[:-1]:
            got = across(passed[c][n])
            before = picked(halves, rows, widths, (c,), marks, [got], before)
        here, *there = across(passed[-1][n])
        near.append((here, before))
        far.append(there)
    settled = settle(halves, widths, utility.reshape(rows, states), marks, own, near)
    out = finish(halves, widths, marks, settled, far)
    return out.reshape(value_now.shape)


def solution(mesh):
    sizes = (mesh.shape["dst"], mesh.shape["org"], mesh.shape["st"])

    def body(*args):
        return on_device(sizes, *args)

    return jax.shard_map(
        body,
        mesh=mesh,
        in_specs=(
            P(("draws", "dst"), "org", None, "st"),
            P(("draws", "dst"), "org", None, "st"),
            P("draws", "org", None, "dst", None),
            P(),
            P(),
            P(),
        ),
        out_specs=P(("draws", "dst"), "org", None, "st"),
        check_vma=False,
    )
```
